32 devices in a mesh: shot: 8 (over z, y), surf: 4 (over x, core).
Axes of the slice: x: 2, y: 2, z: 4, core: 2. Of those that a mesh axis runs over, the one named last changes fastest.
Arguments:
- traces: bfloat16 [64, 1024, 2048], P('shot', 'surf'), may hold values from -6 to 6
- rec_point: int32 [1024], P('surf'), may hold values from 0 to 1023, as said below
- plan: int32 [8], replicated, may hold values from 0 to 7, each once
- green_blocks: bfloat16 [2, 32, 1024, 1024], P(None, 'shot', 'surf'), may hold values from -0.1875 to 0.1875
Outputs:
- multiples: float32 [2, 16, 64, 1024], P(None, None, 'shot', 'surf')
The draws below stay inside these ranges and needn't reach their ends.
Inputs may be any that keep to these rules, and one draw needn't show every extreme that they name: `plan`: each block index appears once; the first 4 entries are used. `rec_point`: receiver r and its surface point p lie in the same one of the equal groups of 256 receivers and 256 surface points, counted in order: p // 256 == r // 256.
All inputs are finite; a program needn't handle non-finite values.
Results may differ from the reference program's by a relative error of at most 0.0029.
Values may be sent and summed in bfloat16 or wider, within the bound.
A program may use at most 128 MiB of HBM per device.

```python
import jax
import jax.numpy as jnp
from jax import lax

S_DEV = 8
R = 1024
X = 1024
T_SIZE = 2048
FB = 4
STEPS = 4
SHOTS = 64
BAND = 32
FREQS = 16
R_DEV = 256
X_DEV = 256
N_SHOT = 8


def draw_rec_point(key, part):
    receiver_groups = jnp.arange(R, dtype=jnp.int32) // R_DEV
    offsets = jax.random.randint(key, (R,), 0, X_DEV, dtype=jnp.int32)
    return (receiver_groups * X_DEV + offsets).astype(jnp.int32)


def shard_levels(rng, extent, pieces, low, top_value):
    gain = 1.0
    for position, blocks in pieces:
        heights = jax.random.uniform(jax.random.fold_in(jax.random.fold_in(rng, 6), position), (blocks,), jnp.float32, low / len(pieces), top_value / len(pieces))
        gain = gain * jnp.repeat(jnp.exp(heights), extent[position] // blocks).reshape((-1,) + (1,) * (len(extent) - 1 - position))
    return gain


def noise(own_key, dims, scale, limit, shards=(), held_as=jnp.bfloat16):
    gain = shard_levels(own_key, dims, shards, -0.22, 0.18) if shards else 1.0
    drawn = jax.random.normal(own_key, dims, jnp.float32) * scale * gain
    return jnp.minimum(jnp.maximum(drawn, -limit), limit).astype(held_as)


def setup_inputs(seed: int = 0) -> dict:
    keys = jax.random.split(jax.random.key(seed), 5)
    traces = noise(keys[0], (SHOTS, R, T_SIZE), 1.0, 6.0, ((0, 8), (1, 4)))
    rec_point = draw_rec_point(jax.random.fold_in(keys[4], 71), 0)
    plan = jax.random.permutation(keys[2], N_SHOT).astype(jnp.int32)
    green_blocks = noise(keys[3], (2, BAND, X, R), X ** -0.5, 0.1875, ((1, 8), (2, 4)))
    return dict(traces=traces, rec_point=rec_point, plan=plan, green_blocks=green_blocks)


def fourier_basis_table(freq_bins):
    times = jnp.arange(T_SIZE, dtype=jnp.int32)
    phases = freq_bins[None, :] * times[:, None] % T_SIZE
    angles = phases.astype(jnp.float32) * (2.0 * jnp.pi / T_SIZE)
    scaling = 1.0 / jnp.sqrt(jnp.float32(T_SIZE))
    return jnp.concatenate([jnp.cos(angles), -jnp.sin(angles)], axis=1) * scaling

def reference(traces, rec_point, plan, green_blocks):
    blocks = plan[:STEPS].astype(jnp.int32)
    frequency_band_rows = (blocks[:, None] * FB + jnp.arange(FB, dtype=jnp.int32)[None, :]).reshape(-1)
    freq_bins = frequency_band_rows + 4
    table = fourier_basis_table(freq_bins)
    grouped = traces.reshape(SHOTS // S_DEV, S_DEV, R, T_SIZE)

    def one_group(shot_rows):
        moved = jnp.transpose(shot_rows, (1, 0, 2)).astype(jnp.float32)
        binned = jax.ops.segment_sum(moved, rec_point, num_segments=X)
        flat = binned.reshape(X * S_DEV, T_SIZE)
        return jnp.dot(flat, table, precision=lax.Precision.HIGHEST).reshape(X, S_DEV, 2 * FREQS)
    spectra = lax.map(one_group, grouped)
    spectra = jnp.transpose(spectra, (1, 0, 2, 3)).reshape(X, SHOTS, 2, FREQS)
    spectra = spectra.astype(jnp.bfloat16).astype(jnp.float32)
    spectra = jnp.transpose(spectra, (2, 3, 1, 0))
    green = green_blocks[:, frequency_band_rows].astype(jnp.float32)
    real_part = jnp.einsum('qsx,qxr->qsr', spectra[0], green[0]) - jnp.einsum('qsx,qxr->qsr', spectra[1], green[1])
    imag_part = jnp.einsum('qsx,qxr->qsr', spectra[0], green[1]) + jnp.einsum('qsx,qxr->qsr', spectra[1], green[0])
    return jnp.stack([real_part, imag_part])
```

```python
import functools

import jax
import jax.numpy as jnp
import numpy as np
from jax import lax
from jax.experimental import pallas as pl
from jax.experimental.pallas import tpu as pltpu
from jax.sharding import PartitionSpec as P

T_SIZE = 2048
FB = 4
STEPS = 4
FIRST_BIN = 4


def basis_table(block_count):
    bins = FIRST_BIN + np.arange(block_count * FB)
    phases = (bins[None, :] * np.arange(T_SIZE)[:, None]) % T_SIZE
    angles = phases * (2.0 * np.pi / T_SIZE)
    table = np.stack([np.cos(angles), -np.sin(angles)], axis=2) / np.sqrt(T_SIZE)
    table = table.reshape(T_SIZE, -1).astype(np.float32)
    high = table.astype(jnp.bfloat16)
    low = (table - high.astype(np.float32)).astype(jnp.bfloat16)
    return np.concatenate([high, low], axis=1)


def kernel(
    n_shot, n_surf,
    plan_ref, rec_ref, table_hbm, traces_hbm, green_hbm,
    out_ref,
    table, traces, green, spec32, outgoing, incoming,
    part, core_in, half_out, half_in, ret_out, ret_in,
    load_sem, trace_sem, fwd_send, fwd_recv, core_send, core_recv,
    surf_send, surf_recv, ret_send, ret_recv,
):
    me = lax.axis_index("shot")
    surf = lax.axis_index("surf")
    core = lax.rem(surf, 2)
    row = surf // 2
    n_rows = n_surf // 2
    shots, r_dev, _ = traces.shape
    x_dev = green.shape[2]
    cols = spec32.shape[1]
    mesh_id = pl.DeviceIdType.MESH

    load_table = pltpu.make_async_copy(table_hbm, table, load_sem.at[0])
    load_table.start()
    for s in range(shots):
        pltpu.make_async_copy(traces_hbm.at[s], traces.at[s], trace_sem.at[s]).start()
    load_green = pltpu.make_async_copy(green_hbm, green, load_sem.at[1])
    load_green.start()

    barrier = pltpu.get_barrier_semaphore()
    for d in range(1, n_shot):
        pl.semaphore_signal(
            barrier, inc=1, device_id=(lax.rem(me + d, n_shot), surf), device_id_type=mesh_id
        )
    pl.semaphore_signal(
        barrier, inc=1, device_id=(me, row * 2 + 1 - core), device_id_type=mesh_id
    )
    for d in range(1, n_rows):
        pl.semaphore_signal(
            barrier, inc=1, device_id=(me, lax.rem(row + d, n_rows) * 2 + core),
            device_id_type=mesh_id,
        )

    local = rec_ref[...] - surf * x_dev
    hot = (lax.broadcasted_iota(jnp.int32, (x_dev, r_dev), 0) == local).astype(jnp.float32)
    hot = hot.astype(jnp.bfloat16)
    load_table.wait()

    def one_shot(s, carry):
        pltpu.make_async_copy(traces_hbm.at[s], traces.at[s], trace_sem.at[s]).wait()
        both = jnp.dot(traces[s], table[...], preferred_element_type=jnp.float32).T
        value = both[:cols] + both[cols:]
        high = value.astype(jnp.bfloat16)
        low = (value - high.astype(jnp.float32)).astype(jnp.bfloat16)
        split = jnp.concatenate([high, low], axis=0)
        moved = lax.dot_general(
            split, hot, (((1,), (1,)), ((), ())), preferred_element_type=jnp.float32
        )
        spec32[s] = moved[:cols] + moved[cols:]
        return carry

    lax.fori_loop(0, shots, one_shot, 0)
    outgoing[...] = jnp.swapaxes(spec32[...], 0, 1).reshape(outgoing.shape).astype(jnp.bfloat16)

    pl.semaphore_wait(barrier, (n_shot - 1) + 1 + (n_rows - 1))

    sends = []
    forward = []
    for d in range(1, n_shot):
        to = lax.rem(me + d, n_shot)
        copy = pltpu.make_async_remote_copy(
            outgoing.at[to], incoming.at[me], fwd_send.at[d], fwd_recv.at[d],
            device_id=(to, surf), device_id_type=mesh_id,
        )
        copy.start()
        forward.append(copy)
    incoming[me] = outgoing[me]
    load_green.wait()
    for copy in forward:
        copy.wait_recv()
    sends += forward

    core_copies, surf_copies, ret_copies = {}, {}, []
    block = 2 * shots

    def multiply(j):
        values = incoming[:, j * block:(j + 1) * block, :].reshape(n_shot * block, x_dev)
        for q in range(n_surf):
            span = slice(q * r_dev, (q + 1) * r_dev)
            by_re = jnp.dot(values, green[0, j, :, span], preferred_element_type=jnp.float32)
            by_im = jnp.dot(values, green[1, j, :, span], preferred_element_type=jnp.float32)
            by_re = by_re.reshape(n_shot, 2, shots, r_dev)
            by_im = by_im.reshape(n_shot, 2, shots, r_dev)
            part[j, q % 2, q // 2, :, 0] = by_re[:, 0] - by_im[:, 1]
            part[j, q % 2, q // 2, :, 1] = by_im[:, 0] + by_re[:, 1]
        copy = pltpu.make_async_remote_copy(
            part.at[j, 1 - core], core_in.at[j], core_send.at[j], core_recv.at[j],
            device_id=(me, row * 2 + 1 - core), device_id_type=mesh_id,
        )
        copy.start()
        core_copies[j] = copy

    def cross(j):
        core_copies[j].wait_recv()
        surf_copies[j] = []
        for d in range(1, n_rows):
            to = lax.rem(row + d, n_rows)
            total = part[j, core, to] + core_in[j, to]
            half_out[j, d - 1] = total.reshape(n_shot, block, r_dev).astype(jnp.bfloat16)
            copy = pltpu.make_async_remote_copy(
                half_out.at[j, d - 1], half_in.at[j, d - 1],
                surf_send.at[j, d - 1], surf_recv.at[j, d - 1],
                device_id=(me, to * 2 + core), device_id_type=mesh_id,
            )
            copy.start()
            surf_copies[j].append(copy)

    def give_back(j):
        total = (part[j, core, row] + core_in[j, row]).reshape(n_shot, block, r_dev)
        for d in range(1, n_rows):
            surf_copies[j][d - 1].wait_recv()
            total = total + half_in[j, d - 1].astype(jnp.float32)
        ret_out[j] = total.astype(jnp.bfloat16)
        for d in range(1, n_shot):
            to = lax.rem(me + d, n_shot)
            copy = pltpu.make_async_remote_copy(
                ret_out.at[j, to], ret_in.at[j, me],
                ret_send.at[j, d], ret_recv.at[j, d],
                device_id=(to, surf), device_id_type=mesh_id,
            )
            copy.start()
            ret_copies.append(copy)
        ret_in[j, me] = ret_out[j, me]

    for t in range(FB + 2):
        if t < FB:
            multiply(t)
        if 0 <= t - 1 < FB:
            cross(t - 1)
        if 0 <= t - 2 < FB:
            give_back(t - 2)

    for copy in ret_copies:
        copy.wait_recv()
    for k in range(STEPS):
        chosen = plan_ref[k]
        for j in range(FB):
            value = ret_in[j, chosen].astype(jnp.float32)
            out_ref[0, k * FB + j] = value[:shots]
            out_ref[1, k * FB + j] = value[shots:]

    for copy in sends:
        copy.wait_send()
    for j in range(FB):
        core_copies[j].wait_send()
        for copy in surf_copies[j]:
            copy.wait_send()
    for copy in ret_copies:
        copy.wait_send()


def solution(mesh):
    n_shot, n_surf = mesh.shape["shot"], mesh.shape["surf"]
    n_rows = n_surf // 2
    table = basis_table(n_shot)

    def body(traces, rec_point, plan, green):
        shots, r_dev, _ = traces.shape
        x_dev = green.shape[2]
        block = 2 * shots
        cols = n_shot * FB * 2
        bf16, f32 = jnp.bfloat16, jnp.float32
        dma = pltpu.SemaphoreType.DMA
        whole = pl.BlockSpec(memory_space=pl.ANY)
        return pl.pallas_call(
            functools.partial(kernel, n_shot, n_surf),
            out_shape=jax.ShapeDtypeStruct((2, STEPS * FB, shots, r_dev), f32),
            in_specs=[
                pl.BlockSpec(memory_space=pltpu.SMEM),
                pl.BlockSpec(memory_space=pltpu.VMEM),
                whole, whole, whole,
            ],
            out_specs=pl.BlockSpec(memory_space=pltpu.VMEM),
            scratch_shapes=[
                pltpu.VMEM(table.shape, bf16),
                pltpu.VMEM(traces.shape, bf16),
                pltpu.VMEM(green.shape, bf16),
                pltpu.VMEM((shots, cols, x_dev), f32),
                pltpu.VMEM((n_shot, FB * block, x_dev), bf16),
                pltpu.VMEM((n_shot, FB * block, x_dev), bf16),
                pltpu.VMEM((FB, 2, n_rows, n_shot, 2, shots, r_dev), f32),
                pltpu.VMEM((FB, n_rows, n_shot, 2, shots, r_dev), f32),
                pltpu.VMEM((FB, n_rows - 1, n_shot, block, r_dev), bf16),
                pltpu.VMEM((FB, n_rows - 1, n_shot, block, r_dev), bf16),
                pltpu.VMEM((FB, n_shot, block, r_dev), bf16),
                pltpu.VMEM((FB, n_shot, block, r_dev), bf16),
                dma((2,)),
                dma((shots,)),
                dma((n_shot,)), dma((n_shot,)),
                dma((FB,)), dma((FB,)),
                dma((FB, n_rows)), dma((FB, n_rows)),
                dma((FB, n_shot)), dma((FB, n_shot)),
            ],
            compiler_params=pltpu.CompilerParams(
                collective_id=0, has_side_effects=True, vmem_limit_bytes=48 << 20
            ),
        )(plan, rec_point.reshape(1, r_dev), jnp.asarray(table), traces, green)

    in_specs = (P("shot", "surf", None), P("surf"), P(), P(None, "shot", "surf", None))
    out_specs = P(None, None, "shot", "surf")
    return jax.shard_map(body, mesh=mesh, in_specs=in_specs, out_specs=out_specs, check_vma=False)
```

```python
import functools

import jax
import jax.numpy as jnp
import numpy as np
from jax import lax
from jax.experimental import pallas as pl
from jax.experimental.pallas import tpu as pltpu
from jax.sharding import PartitionSpec as P

T_SIZE = 2048
FB = 4
STEPS = 4
FIRST_BIN = 4
CHUNKS = 4
SKEW = 3


def basis_table(block_count):
    bins = FIRST_BIN + np.arange(block_count * FB)
    phases = (bins[None, :] * np.arange(T_SIZE)[:, None]) % T_SIZE
    angles = phases * (2.0 * np.pi / T_SIZE)
    table = np.stack([np.cos(angles), -np.sin(angles)], axis=2) / np.sqrt(T_SIZE)
    table = table.reshape(T_SIZE, -1).astype(np.float32)
    high = table.astype(jnp.bfloat16)
    low = (table - high.astype(np.float32)).astype(jnp.bfloat16)
    return np.concatenate([high, low], axis=1)


def kernel(
    n_shot, n_surf,
    plan_hbm, rec_hbm, table_hbm, traces_hbm, green_hbm,
    out_ref,
    plan_ref, rec_ref, table, traces, green, spec32, outgoing, incoming,
    part, core_in, half_out, half_in, ret_out, ret_in,
    load_sem, trace_sem, fwd_send, fwd_recv, core_send, core_recv,
    surf_send, surf_recv, ret_send, ret_recv,
):
    me = lax.axis_index("shot")
    surf = lax.axis_index("surf")
    core = lax.rem(surf, 2)
    row = surf // 2
    n_rows = n_surf // 2
    shots, r_dev, _ = traces.shape
    x_dev = green.shape[2]
    cols = spec32.shape[1]
    mesh_id = pl.DeviceIdType.MESH

    load_table = pltpu.make_async_copy(table_hbm, table, load_sem.at[0])
    load_rec = pltpu.make_async_copy(rec_hbm, rec_ref, load_sem.at[2])
    load_rec.start()
    load_table.start()
    for s in range(shots):
        pltpu.make_async_copy(traces_hbm.at[s], traces.at[s], trace_sem.at[s]).start()
    load_green = pltpu.make_async_copy(green_hbm, green, load_sem.at[1])
    load_green.start()
    load_plan = pltpu.make_async_copy(plan_hbm, plan_ref, load_sem.at[3])
    load_plan.start()

    barrier = pltpu.get_barrier_semaphore()
    for d in range(1, n_shot):
        pl.semaphore_signal(
            barrier, inc=1, device_id=(lax.rem(me + d, n_shot), surf), device_id_type=mesh_id
        )
    pl.semaphore_signal(
        barrier, inc=1, device_id=(me, row * 2 + 1 - core), device_id_type=mesh_id
    )
    for d in range(1, n_rows):
        pl.semaphore_signal(
            barrier, inc=1, device_id=(me, lax.rem(row + d, n_rows) * 2 + core),
            device_id_type=mesh_id,
        )

    load_rec.wait()
    local = rec_ref[...] - surf * x_dev
    hot = (lax.broadcasted_iota(jnp.int32, (x_dev, r_dev), 0) == local).astype(jnp.float32)
    hot = hot.astype(jnp.bfloat16)
    load_table.wait()

    def one_shot(s, carry):
        pltpu.make_async_copy(traces_hbm.at[s], traces.at[s], trace_sem.at[s]).wait()
        both = jnp.dot(traces[s], table[...], preferred_element_type=jnp.float32).T
        value = both[:cols] + both[cols:]
        high = value.astype(jnp.bfloat16)
        low = (value - high.astype(jnp.float32)).astype(jnp.bfloat16)
        split = jnp.concatenate([high, low], axis=0)
        moved = lax.dot_general(
            split, hot, (((1,), (1,)), ((), ())), preferred_element_type=jnp.float32
        )
        spec32[s] = moved[:cols] + moved[cols:]
        return carry

    lax.fori_loop(0, shots, one_shot, 0)
    outgoing[...] = jnp.swapaxes(spec32[...], 0, 1).reshape(outgoing.shape).astype(jnp.bfloat16)

    pl.semaphore_wait(barrier, (n_shot - 1) + 1 + (n_rows - 1))

    block = 2 * shots
    width = FB // CHUNKS
    order = sorted(range(1, n_shot), key=lambda d: abs(2 * d - n_shot))
    forward = {}
    for c in range(CHUNKS):
        rows = pl.ds(c * width * block, width * block)
        for d in order:
            to = lax.rem(me + d, n_shot)
            copy = pltpu.make_async_remote_copy(
                outgoing.at[to, rows], incoming.at[me, rows],
                fwd_send.at[c, d], fwd_recv.at[c, d],
                device_id=(to, surf), device_id_type=mesh_id,
            )
            copy.start()
            forward[c, d] = copy
    incoming[me] = outgoing[me]
    load_green.wait()

    core_copies, surf_copies, ret_copies = {}, {}, []

    def multiply(j):
        if j % width == 0:
            for d in order:
                forward[j // width, d].wait_recv()
        values = incoming[:, j * block:(j + 1) * block, :].reshape(n_shot * block, x_dev)
        for q in range(n_surf):
            span = slice(q * r_dev, (q + 1) * r_dev)
            by_re = jnp.dot(values, green[0, j, :, span], preferred_element_type=jnp.float32)
            by_im = jnp.dot(values, green[1, j, :, span], preferred_element_type=jnp.float32)
            by_re = by_re.reshape(n_shot, 2, shots, r_dev)
            by_im = by_im.reshape(n_shot, 2, shots, r_dev)
            part[j, q % 2, q // 2, :, 0] = by_re[:, 0] - by_im[:, 1]
            part[j, q % 2, q // 2, :, 1] = by_im[:, 0] + by_re[:, 1]
        copy = pltpu.make_async_remote_copy(
            part.at[j, 1 - core], core_in.at[j], core_send.at[j], core_recv.at[j],
            device_id=(me, row * 2 + 1 - core), device_id_type=mesh_id,
        )
        copy.start()
        core_copies[j] = copy

    def cross(j):
        core_copies[j].wait_recv()
        surf_copies[j] = []
        for d in range(1, n_rows):
            to = lax.rem(row + d, n_rows)
            total = part[j, core, to] + core_in[j, to]
            half_out[j, d - 1] = total.reshape(n_shot, block, r_dev).astype(jnp.bfloat16)
            copy = pltpu.make_async_remote_copy(
                half_out.at[j, d - 1], half_in.at[j, d - 1],
                surf_send.at[j, d - 1], surf_recv.at[j, d - 1],
                device_id=(me, to * 2 + core), device_id_type=mesh_id,
            )
            copy.start()
            surf_copies[j].append(copy)

    def give_back(j):
        total = (part[j, core, row] + core_in[j, row]).reshape(n_shot, block, r_dev)
        for d in range(1, n_rows):
            surf_copies[j][d - 1].wait_recv()
            total = total + half_in[j, d - 1].astype(jnp.float32)
        ret_out[j] = total.astype(jnp.bfloat16)
        for d in order:
            to = lax.rem(me + d, n_shot)
            copy = pltpu.make_async_remote_copy(
                ret_out.at[j, to], ret_in.at[j, me],
                ret_send.at[j, d], ret_recv.at[j, d],
                device_id=(to, surf), device_id_type=mesh_id,
            )
            copy.start()
            ret_copies.append(copy)
        ret_in[j, me] = ret_out[j, me]

    for t in range(FB + SKEW):
        if t < FB:
            multiply(t)
        if 0 <= t - 1 < FB:
            cross(t - 1)
        if 0 <= t - SKEW < FB:
            give_back(t - SKEW)

    for copy in ret_copies:
        copy.wait_recv()
    load_plan.wait()
    for k in range(STEPS):
        chosen = plan_ref[k]
        for j in range(FB):
            value = ret_in[j, chosen].astype(jnp.float32)
            out_ref[0, k * FB + j] = value[:shots]
            out_ref[1, k * FB + j] = value[shots:]

    for copy in forward.values():
        copy.wait_send()
    for j in range(FB):
        core_copies[j].wait_send()
        for copy in surf_copies[j]:
            copy.wait_send()
    for copy in ret_copies:
        copy.wait_send()


def solution(mesh):
    n_shot, n_surf = mesh.shape["shot"], mesh.shape["surf"]
    n_rows = n_surf // 2
    table = basis_table(n_shot)

    def body(traces, rec_point, plan, green):
        shots, r_dev, _ = traces.shape
        x_dev = green.shape[2]
        block = 2 * shots
        cols = n_shot * FB * 2
        bf16, f32 = jnp.bfloat16, jnp.float32
        dma = pltpu.SemaphoreType.DMA
        whole = pl.BlockSpec(memory_space=pltpu.HBM)
        return pl.pallas_call(
            functools.partial(kernel, n_shot, n_surf),
            out_shape=jax.ShapeDtypeStruct((2, STEPS * FB, shots, r_dev), f32),
            in_specs=[whole] * 5,
            out_specs=pl.BlockSpec(memory_space=pltpu.VMEM),
            scratch_shapes=[
                pltpu.SMEM(plan.shape, jnp.int32),
                pltpu.VMEM((1, r_dev), jnp.int32),
                pltpu.VMEM(table.shape, bf16),
                pltpu.VMEM(traces.shape, bf16),
                pltpu.VMEM(green.shape, bf16),
                pltpu.VMEM((shots, cols, x_dev), f32),
                pltpu.VMEM((n_shot, FB * block, x_dev), bf16),
                pltpu.VMEM((n_shot, FB * block, x_dev), bf16),
                pltpu.VMEM((FB, 2, n_rows, n_shot, 2, shots, r_dev), f32),
                pltpu.VMEM((FB, n_rows, n_shot, 2, shots, r_dev), f32),
                pltpu.VMEM((FB, n_rows - 1, n_shot, block, r_dev), bf16),
                pltpu.VMEM((FB, n_rows - 1, n_shot, block, r_dev), bf16),
                pltpu.VMEM((FB, n_shot, block, r_dev), bf16),
                pltpu.VMEM((FB, n_shot, block, r_dev), bf16),
                dma((4,)),
                dma((shots,)),
                dma((CHUNKS, n_shot)), dma((CHUNKS, n_shot)),
                dma((FB,)), dma((FB,)),
                dma((FB, n_rows)), dma((FB, n_rows)),
                dma((FB, n_shot)), dma((FB, n_shot)),
            ],
            compiler_params=pltpu.CompilerParams(
                collective_id=0, has_side_effects=True, vmem_limit_bytes=60 << 20
            ),
        )(plan, rec_point.reshape(1, r_dev), jnp.asarray(table), traces, green)

    in_specs = (P("shot", "surf", None), P("surf"), P(), P(None, "shot", "surf", None))
    out_specs = P(None, None, "shot", "surf")
    return jax.shard_map(body, mesh=mesh, in_specs=in_specs, out_specs=out_specs, check_vma=False)
```

```python
import functools

import jax
import jax.numpy as jnp
import numpy as np
from jax import lax
from jax.experimental import pallas as pl
from jax.experimental.pallas import tpu as pltpu
from jax.sharding import PartitionSpec as P

T_SIZE = 2048
FB = 4
STEPS = 4
FIRST_BIN = 4
CHUNKS = 4
SKEW = 3


def basis_table(block_count):
    bins = FIRST_BIN + np.arange(block_count * FB)
    phases = (bins[None, :] * np.arange(T_SIZE)[:, None]) % T_SIZE
    angles = phases * (2.0 * np.pi / T_SIZE)
    table = np.stack([np.cos(angles), -np.sin(angles)], axis=2) / np.sqrt(T_SIZE)
    table = table.reshape(T_SIZE, -1).astype(np.float32)
    high = table.astype(jnp.bfloat16)
    low = (table - high.astype(np.float32)).astype(jnp.bfloat16)
    return np.concatenate([high, low], axis=1)


def kernel(
    n_shot, n_surf,
    plan_hbm, rec_hbm, table_hbm, traces_hbm, green_hbm,
    out_ref,
    plan_ref, rec_ref, table, traces, green, spec32, outgoing, incoming,
    part, core_in, half_out, half_in, ret_out, ret_in,
    load_sem, trace_sem, fwd_send, fwd_recv, core_send, core_recv,
    surf_send, surf_recv, ret_send, ret_recv,
):
    me = lax.axis_index("shot")
    surf = lax.axis_index("surf")
    core = lax.rem(surf, 2)
    row = surf // 2
    n_rows = n_surf // 2
    shots, r_dev, _ = traces.shape
    x_dev = green.shape[2]
    cols = spec32.shape[1]
    mesh_id = pl.DeviceIdType.MESH

    order = sorted(range(1, n_shot), key=lambda d: abs(2 * d - n_shot))
    barrier = pltpu.get_barrier_semaphore()
    for d in order:
        pl.semaphore_signal(
            barrier, inc=1, device_id=(lax.rem(me + d, n_shot), surf), device_id_type=mesh_id
        )
    pl.semaphore_signal(
        barrier, inc=1, device_id=(me, row * 2 + 1 - core), device_id_type=mesh_id
    )
    for d in range(1, n_rows):
        pl.semaphore_signal(
            barrier, inc=1, device_id=(me, lax.rem(row + d, n_rows) * 2 + core),
            device_id_type=mesh_id,
        )

    load_table = pltpu.make_async_copy(table_hbm, table, load_sem.at[0])
    load_rec = pltpu.make_async_copy(rec_hbm, rec_ref, load_sem.at[2])
    load_rec.start()
    load_table.start()
    for s in range(3):
        pltpu.make_async_copy(traces_hbm.at[s], traces.at[s], trace_sem.at[s]).start()
    load_green = pltpu.make_async_copy(green_hbm, green, load_sem.at[1])
    load_plan = pltpu.make_async_copy(plan_hbm, plan_ref, load_sem.at[3])
    load_plan.start()

    load_rec.wait()
    local = rec_ref[...] - surf * x_dev
    hot = (lax.broadcasted_iota(jnp.int32, (x_dev, r_dev), 0) == local).astype(jnp.float32)
    hot = hot.astype(jnp.bfloat16)
    load_table.wait()

    def one_shot(s, carry):
        pltpu.make_async_copy(traces_hbm.at[s], traces.at[s], trace_sem.at[s]).wait()
        if s + 3 < shots:
            pltpu.make_async_copy(traces_hbm.at[s + 3], traces.at[s + 3], trace_sem.at[s + 3]).start()
        elif s + 3 == shots:
            load_green.start()
        both = jnp.dot(traces[s], table[...], preferred_element_type=jnp.float32).T
        value = both[:cols] + both[cols:]
        high = value.astype(jnp.bfloat16)
        low = (value - high.astype(jnp.float32)).astype(jnp.bfloat16)
        split = jnp.concatenate([high, low], axis=0)
        moved = lax.dot_general(
            split, hot, (((1,), (1,)), ((), ())), preferred_element_type=jnp.float32
        )
        spec32[s] = moved[:cols] + moved[cols:]
        return carry

    for s in range(shots):
        one_shot(s, 0)
    outgoing[...] = jnp.swapaxes(spec32[...], 0, 1).reshape(outgoing.shape).astype(jnp.bfloat16)

    pl.semaphore_wait(barrier, (n_shot - 1) + 1 + (n_rows - 1))

    block = 2 * shots
    width = FB // CHUNKS
    forward = {}
    for c in range(CHUNKS):
        rows = pl.ds(c * width * block, width * block)
        for d in order:
            to = lax.rem(me + d, n_shot)
            copy = pltpu.make_async_remote_copy(
                outgoing.at[to, rows], incoming.at[me, rows],
                fwd_send.at[c, d], fwd_recv.at[c, d],
                device_id=(to, surf), device_id_type=mesh_id,
            )
            copy.start()
            forward[c, d] = copy
    incoming[me] = outgoing[me]
    load_green.wait()

    core_copies, surf_copies, ret_copies = {}, {}, []

    def multiply(j):
        if j % width == 0:
            for d in order:
                forward[j // width, d].wait_recv()
        values = incoming[:, j * block:(j + 1) * block, :].reshape(n_shot * block, x_dev)
        for q in range(n_surf):
            span = slice(q * r_dev, (q + 1) * r_dev)
            by_re = jnp.dot(values, green[0, j, :, span], preferred_element_type=jnp.float32)
            by_im = jnp.dot(values, green[1, j, :, span], preferred_element_type=jnp.float32)
            by_re = by_re.reshape(n_shot, 2, shots, r_dev)
            by_im = by_im.reshape(n_shot, 2, shots, r_dev)
            part[j, q % 2, q // 2, :, 0] = by_re[:, 0] - by_im[:, 1]
            part[j, q % 2, q // 2, :, 1] = by_im[:, 0] + by_re[:, 1]
        copy = pltpu.make_async_remote_copy(
            part.at[j, 1 - core], core_in.at[j], core_send.at[j], core_recv.at[j],
            device_id=(me, row * 2 + 1 - core), device_id_type=mesh_id,
        )
        copy.start()
        core_copies[j] = copy

    def cross(j):
        core_copies[j].wait_recv()
        surf_copies[j] = []
        for d in range(1, n_rows):
            to = lax.rem(row + d, n_rows)
            total = part[j, core, to] + core_in[j, to]
            half_out[j, d - 1] = total.reshape(n_shot, block, r_dev).astype(jnp.bfloat16)
            copy = pltpu.make_async_remote_copy(
                half_out.at[j, d - 1], half_in.at[j, d - 1],
                surf_send.at[j, d - 1], surf_recv.at[j, d - 1],
                device_id=(me, to * 2 + core), device_id_type=mesh_id,
            )
            copy.start()
            surf_copies[j].append(copy)

    def give_back(j):
        total = (part[j, core, row] + core_in[j, row]).reshape(n_shot, block, r_dev)
        for d in range(1, n_rows):
            surf_copies[j][d - 1].wait_recv()
            total = total + half_in[j, d - 1].astype(jnp.float32)
        ret_out[j] = total.astype(jnp.bfloat16)
        for d in order:
            to = lax.rem(me + d, n_shot)
            copy = pltpu.make_async_remote_copy(
                ret_out.at[j, to], ret_in.at[j, me],
                ret_send.at[j, d], ret_recv.at[j, d],
                device_id=(to, surf), device_id_type=mesh_id,
            )
            copy.start()
            ret_copies.append(copy)
        ret_in[j, me] = ret_out[j, me]

    for t in range(FB + SKEW):
        if t < FB:
            multiply(t)
        if 0 <= t - 1 < FB:
            cross(t - 1)
        if 0 <= t - SKEW < FB:
            give_back(t - SKEW)

    for copy in ret_copies:
        copy.wait_recv()
    load_plan.wait()
    for k in range(STEPS):
        chosen = plan_ref[k]
        for j in range(FB):
            out_ref[k * FB + j] = ret_in[j, chosen]

    for copy in forward.values():
        copy.wait_send()
    for j in range(FB):
        core_copies[j].wait_send()
        for copy in surf_copies[j]:
            copy.wait_send()
    for copy in ret_copies:
        copy.wait_send()


def solution(mesh):
    n_shot, n_surf = mesh.shape["shot"], mesh.shape["surf"]
    n_rows = n_surf // 2
    table = basis_table(n_shot)

    def body(traces, rec_point, plan, green):
        shots, r_dev, _ = traces.shape
        x_dev = green.shape[2]
        block = 2 * shots
        cols = n_shot * FB * 2
        bf16, f32 = jnp.bfloat16, jnp.float32
        dma = pltpu.SemaphoreType.DMA
        whole = pl.BlockSpec(memory_space=pltpu.HBM)
        chosen = pl.pallas_call(
            functools.partial(kernel, n_shot, n_surf),
            out_shape=jax.ShapeDtypeStruct((STEPS * FB, block, r_dev), bf16),
            in_specs=[whole] * 5,
            out_specs=pl.BlockSpec(memory_space=pltpu.VMEM),
            scratch_shapes=[
                pltpu.SMEM(plan.shape, jnp.int32),
                pltpu.VMEM((1, r_dev), jnp.int32),
                pltpu.VMEM(table.shape, bf16),
                pltpu.VMEM(traces.shape, bf16),
                pltpu.VMEM(green.shape, bf16),
                pltpu.VMEM((shots, cols, x_dev), f32),
                pltpu.VMEM((n_shot, FB * block, x_dev), bf16),
                pltpu.VMEM((n_shot, FB * block, x_dev), bf16),
                pltpu.VMEM((FB, 2, n_rows, n_shot, 2, shots, r_dev), f32),
                pltpu.VMEM((FB, n_rows, n_shot, 2, shots, r_dev), f32),
                pltpu.VMEM((FB, n_rows - 1, n_shot, block, r_dev), bf16),
                pltpu.VMEM((FB, n_rows - 1, n_shot, block, r_dev), bf16),
                pltpu.VMEM((FB, n_shot, block, r_dev), bf16),
                pltpu.VMEM((FB, n_shot, block, r_dev), bf16),
                dma((4,)),
                dma((shots,)),
                dma((CHUNKS, n_shot)), dma((CHUNKS, n_shot)),
                dma((FB,)), dma((FB,)),
                dma((FB, n_rows)), dma((FB, n_rows)),
                dma((FB, n_shot)), dma((FB, n_shot)),
            ],
            compiler_params=pltpu.CompilerParams(
                collective_id=0, has_side_effects=True, vmem_limit_bytes=48 << 20
            ),
        )(*[pltpu.with_memory_space_constraint(v, pltpu.HBM) for v in (plan, rec_point.reshape(1, r_dev), jnp.asarray(table), traces, green)])
        chosen = chosen.reshape(STEPS * FB, 2, shots, r_dev).astype(f32)
        return jnp.swapaxes(chosen, 0, 1)

    in_specs = (P("shot", "surf", None), P("surf"), P(), P(None, "shot", "surf", None))
    out_specs = P(None, None, "shot", "surf")
    return jax.shard_map(body, mesh=mesh, in_specs=in_specs, out_specs=out_specs, check_vma=False)
```
